768 devices in a mesh: orb: 12 (over x, z_lo), sx: 8 (over y), sy: 8 (over z_hi, core).
Axes of the slice: x: 4, y: 8, z: 12 (z_hi: 4, z_lo: 3; z = z_hi * 3 + z_lo), core: 2. Of those that a mesh axis runs over, the one named last changes fastest.
Arguments:
- orbitals: bfloat16 [64, 64, 24576], P('sx', 'sy', 'orb'), may hold values from -6 to 6
- src_owner: int32 [2, 2], replicated, may hold values from 0 to 11
- src_slot: int32 [2, 2], replicated, may hold values from 0 to 63
Outputs:
- exchange_field: float32 [64, 64, 24576], P('sx', 'sy', 'orb')
The draws below stay inside these ranges and needn't reach their ends.
All inputs are finite; a program needn't handle non-finite values.
Results may differ from the reference program's by a relative error of at most 0.0003.
Values may be sent and summed in bfloat16 or wider, within the bound.
A program may use at most 128 MiB of HBM per device.

```python
import jax
import jax.numpy as jnp
from jax import lax

NZ = 32
TGT = 64
SRC = 2
ROUNDS = 2
DEGREE = 4
NX = 64
NY = 64
NORB = 768
N_ORB = 12


def draw_orbitals(key, part):
    key_base = jax.random.fold_in(key, 0)
    array_shape = (NX, NY, NORB * NZ)
    values = jnp.clip(jax.random.normal(key_base, array_shape, jnp.float32), -6.0, 6.0)
    return values.astype(jnp.bfloat16)


def place_ends(result, rng, low, top_value):
    place = [jax.random.randint(jax.random.fold_in(rng, axis), (), 0, length) for axis, length in enumerate(result.shape)]
    main_axis = result.shape.index(max(result.shape))
    beside = place[:main_axis] + [(place[main_axis] + 1) % result.shape[main_axis]] + place[main_axis + 1:]
    return result.at[tuple(place)].set(low).at[tuple(beside)].set(top_value)


def setup_inputs(seed: int = 0) -> dict:
    keys = jax.random.split(jax.random.key(seed), 4)
    return {
        "orbitals": draw_orbitals(jax.random.fold_in(keys[3], 71), 0),
        "src_owner": place_ends(jax.random.randint(keys[1], (ROUNDS, SRC), 0, N_ORB), jax.random.fold_in(keys[1], 1), 0, N_ORB - 1).astype(jnp.int32),
        "src_slot": place_ends(jax.random.randint(keys[2], (ROUNDS, SRC), 0, TGT), jax.random.fold_in(keys[2], 1), 0, TGT - 1).astype(jnp.int32),
    }


cheb_coeffs = (1.021021021021021, -1.7357357357357357, 1.4753753753753754, -1.2540690690690691, 1.0659587087087087)


def screened(field):
    side = jnp.roll(field, -1, 1) + jnp.roll(field, 1, 1)
    side = side + jnp.roll(field, -1, 2) + jnp.roll(field, 1, 2)
    padded = jnp.pad(field, ((0, 0), (0, 0), (0, 0), (1, 1)))
    side = side + padded[..., 2:] + padded[..., :-2]
    return -side / 6.0


def potential(density):
    t_prev = density
    t_cur = screened(density)
    total = cheb_coeffs[0] * t_prev + cheb_coeffs[1] * t_cur
    for order in range(2, DEGREE + 1):
        t_next = 2.0 * screened(t_cur) - t_prev
        total = total + cheb_coeffs[order] * t_next
        t_prev, t_cur = t_cur, t_next
    return total


def reference(orbitals, src_owner, src_slot):
    grid = orbitals.astype(jnp.float32).reshape(NX, NY, NORB, NZ).transpose(2, 0, 1, 3)
    picked = (src_owner * TGT + src_slot).reshape(-1).astype(jnp.int32)
    sources = grid[picked]

    def one_target(target):
        density = sources * target[None]
        return -jnp.sum(potential(density) * sources, axis=0)

    fields = lax.map(one_target, grid)
    return fields.transpose(1, 2, 0, 3).reshape(NX, NY, NORB * NZ)
```

```python
import functools

import jax
import jax.numpy as jnp
from jax import lax
from jax.experimental import pallas as pl
from jax.experimental.pallas import tpu as pltpu
from jax.sharding import PartitionSpec as P

NZ = 32
NSRC = 4
ZLO = 3
LANES = 128
PACK = LANES // NZ
GROUPS = 8
HALO = 4
BLK = 8
EXT = BLK + 2 * HALO
MESH = pl.DeviceIdType.MESH

C = (1.021021021021021, -1.7357357357357357, 1.4753753753753753, -1.254069069069069, 1.0659587087087088)
IN_B = (C[0] - C[2] + C[4], C[1] - 3 * C[3], 2 * C[2] - 8 * C[4], 4 * C[3], 8 * C[4])
IN_S = tuple(a * (-1.0 / 6.0) ** k for k, a in enumerate(IN_B))
LEAD = IN_S[4]
REL = tuple(a / LEAD for a in IN_S)

DIRS = tuple((ax, ay) for ax in (-1, 0, 1) for ay in (-1, 0, 1) if (ax, ay) != (0, 0))


def src_range(a, width):
    return {-1: slice(HALO, HALO + width), 0: slice(HALO, HALO + BLK), 1: slice(HALO + BLK - width, HALO + BLK)}[a]


def dst_range(a, width):
    return {-1: slice(HALO + BLK, HALO + BLK + width), 0: slice(HALO, HALO + BLK), 1: slice(HALO - width, HALO)}[a]


def kernel(
    nx, nsx, nsy,
    owner, slot, orb_hbm, out,
    inb, tall, phi, gx, gz, pp, pt, rho, wa, wb,
    in_sem, xs, xr, zs, zr, ps, pr, hs, hr,
):
    orb = lax.axis_index("orb")
    mx, mz = orb // ZLO, orb % ZLO
    sx, sy = lax.axis_index("sx"), lax.axis_index("sy")

    def near(ax, ay):
        return {"sx": lax.rem(sx + ax + nsx, nsx), "sy": lax.rem(sy + ay + nsy, nsy)}

    def x_peer(d):
        return {"orb": lax.rem(mx + d, nx) * ZLO + mz}

    def z_peer(d):
        return {"orb": mx * ZLO + lax.rem(mz + d, ZLO)}

    load = pltpu.make_async_copy(orb_hbm, inb, in_sem)
    load.start()
    barrier = pltpu.get_barrier_semaphore()
    peers = [near(*d) for d in DIRS] + [x_peer(d) for d in range(1, nx)] + [z_peer(d) for d in range(1, ZLO)]
    for peer in peers:
        pl.semaphore_signal(barrier, inc=1, device_id=peer, device_id_type=MESH)
    load.wait()

    lane = lax.broadcasted_iota(jnp.int32, (BLK, LANES), 1)
    part, cell = lane // NZ, lane % NZ

    cand = jnp.zeros((BLK, BLK, LANES), jnp.float32)
    mine = part + orb * (2 * GROUPS * PACK)
    wanted = [owner[s // 2, s % 2] * (2 * GROUPS * PACK) + slot[s // 2, s % 2] for s in range(NSRC)]
    got = [jnp.zeros((BLK, BLK, LANES), jnp.float32) for s in range(NSRC)]
    for g in range(2 * GROUPS):
        row = inb[:, :, g * LANES : (g + 1) * LANES].astype(jnp.float32)
        for s in range(NSRC):
            got[s] = jnp.where((mine + g * PACK == wanted[s])[None], row, got[s])
    for s in range(NSRC):
        m = got[s] + pltpu.roll(got[s], NZ, 2)
        m = m + pltpu.roll(m, 2 * NZ, 2)
        cand = jnp.where((part == s)[None], m, cand)
    gx[mx] = cand.astype(jnp.bfloat16)

    def relay(x, carry):
        for g in range(2 * GROUPS):
            tall[x, :, g, :] = inb[x, :, g * LANES : (g + 1) * LANES].astype(jnp.float32)
        for h in range(2):
            phi[h, HALO + x, HALO : HALO + BLK] = tall[x, :, h * GROUPS : (h + 1) * GROUPS, :].astype(jnp.bfloat16)
        return carry

    lax.fori_loop(0, BLK, relay, 0)

    pl.semaphore_wait(barrier, len(peers))

    x_copies = [
        pltpu.make_async_remote_copy(gx.at[mx], gx.at[mx], xs.at[d - 1], xr.at[d - 1], device_id=x_peer(d), device_id_type=MESH)
        for d in range(1, nx)
    ]
    for copy in x_copies:
        copy.start()

    def halo_copies(h):
        copies = []
        for k, (ax, ay) in enumerate(DIRS):
            width = HALO - 1 if ax and ay else HALO
            copies.append(
                pltpu.make_async_remote_copy(
                    phi.at[h, src_range(ax, width), src_range(ay, width)],
                    phi.at[h, dst_range(ax, width), dst_range(ay, width)],
                    hs.at[h, k], hr.at[h, k], device_id=near(ax, ay), device_id_type=MESH,
                )
            )
        return copies

    first, second = halo_copies(0), halo_copies(1)
    for copy in first:
        copy.start()

    for copy in x_copies:
        copy.wait_recv()
    mid = gx[0].astype(jnp.float32)
    for x in range(1, nx):
        mid = mid + gx[x].astype(jnp.float32)
    gz[mz] = mid.astype(jnp.bfloat16)
    z_copies = [
        pltpu.make_async_remote_copy(gz.at[mz], gz.at[mz], zs.at[d - 1], zr.at[d - 1], device_id=z_peer(d), device_id_type=MESH)
        for d in range(1, ZLO)
    ]
    for copy in z_copies:
        copy.start()
    for copy in z_copies:
        copy.wait_recv()
    mid = gz[0].astype(jnp.float32)
    for z in range(1, ZLO):
        mid = mid + gz[z].astype(jnp.float32)
    pp[1, HALO : HALO + BLK] = mid.astype(jnp.bfloat16)
    p_copies = [
        pltpu.make_async_remote_copy(
            pp.at[1, src_range(ax, HALO)], pp.at[1 - ay, dst_range(ax, HALO)],
            ps.at[k], pr.at[k], device_id=near(ax, ay), device_id_type=MESH,
        )
        for k, (ax, ay) in enumerate(DIRS)
    ]
    for copy in p_copies:
        copy.start()
    for copy in second:
        copy.start()
    for copy in p_copies:
        copy.wait_recv()

    def expand(x, carry):
        for b in range(3):
            t = pp[b, x].astype(jnp.float32)
            for s in range(NSRC):
                m = jnp.where(part == s, t, 0.0)
                m = m + pltpu.roll(m, NZ, 1)
                m = m + pltpu.roll(m, 2 * NZ, 1)
                pt[s, x, b * BLK : (b + 1) * BLK, :] = m
        return carry

    lax.fori_loop(0, EXT, expand, 0)

    up = (cell != 0).astype(jnp.float32)[None]
    down = (cell != NZ - 1).astype(jnp.float32)[None]

    def level(k, s, src, write):
        n = EXT - 2 * k
        rows = slice(k - 1, k + n + 1)
        inner = slice(k, k + n)

        def step(x, carry):
            diag, here = carry
            after = src(x + 1, rows)
            diag_here = here[: n + 1] + after[1:]
            mid = here[1 : n + 1]
            total = diag + diag_here[:n]
            total = total + (pltpu.roll(mid, 1, 2) * up + pltpu.roll(mid, LANES - 1, 2) * down)
            write(x, total + REL[4 - k] * rho[s, x, inner])
            return diag_here[1:], after

        here = src(k, rows)
        diag = src(k - 1, inner) + here[2:]
        lax.fori_loop(k, k + n, step, (diag, here))

    def half(h):
        lo = h * GROUPS

        def density(x, carry):
            row = phi[h, x].astype(jnp.float32)
            for s in range(NSRC):
                for y in range(EXT):
                    rho[s, x, y] = row[y] * pt[s, x, y + HALO : y + HALO + 1, :]
            tall[x // 2, pl.ds((x % 2) * HALO, HALO), lo : lo + GROUPS, :] = jnp.zeros((HALO, GROUPS, LANES), jnp.float32)
            return carry

        lax.fori_loop(0, EXT, density, 0)

        def source(s, carry):
            def to(ref, k):
                def write(x, value):
                    ref[x, k : EXT - k] = value

                return write

            def finish(x, value):
                for y in range(BLK):
                    term = value[y] * pt[s, x, y + 2 * HALO : y + 2 * HALO + 1, :]
                    tall[x - HALO, y, lo : lo + GROUPS, :] = tall[x - HALO, y, lo : lo + GROUPS, :] + term

            level(1, s, lambda x, r: rho[s, x, r], to(wa, 1))
            level(2, s, lambda x, r: wa[x, r], to(wb, 2))
            level(3, s, lambda x, r: wb[x, r], to(wa, 3))
            level(4, s, lambda x, r: wa[x, r], finish)
            return carry

        lax.fori_loop(0, NSRC, source, 0)

        def store(x, carry):
            for g in range(lo, lo + GROUPS):
                out[x, :, g * LANES : (g + 1) * LANES] = tall[x, :, g, :] * (-LEAD)
            return carry

        lax.fori_loop(0, BLK, store, 0)

    for copy in first:
        copy.wait_recv()
    half(0)
    for copy in second:
        copy.wait_recv()
    half(1)
    for copy in x_copies + z_copies + p_copies + first + second:
        copy.wait_send()


def solution(mesh):
    nx, nsx, nsy = mesh.shape["orb"] // ZLO, mesh.shape["sx"], mesh.shape["sy"]

    def body(orbitals, src_owner, src_slot):
        f32, bf16 = jnp.float32, jnp.bfloat16
        dma = pltpu.SemaphoreType.DMA
        return pl.pallas_call(
            functools.partial(kernel, nx, nsx, nsy),
            out_shape=jax.ShapeDtypeStruct(orbitals.shape, f32),
            in_specs=[
                pl.BlockSpec(memory_space=pltpu.SMEM),
                pl.BlockSpec(memory_space=pltpu.SMEM),
                pl.BlockSpec(memory_space=pl.ANY),
            ],
            out_specs=pl.BlockSpec(memory_space=pltpu.VMEM),
            scratch_shapes=[
                pltpu.VMEM(orbitals.shape, bf16),
                pltpu.VMEM((BLK, BLK, 2 * GROUPS, LANES), f32),
                pltpu.VMEM((2, EXT, EXT, GROUPS, LANES), bf16),
                pltpu.VMEM((nx, BLK, BLK, LANES), bf16),
                pltpu.VMEM((ZLO, BLK, BLK, LANES), bf16),
                pltpu.VMEM((3, EXT, BLK, LANES), bf16),
                pltpu.VMEM((NSRC, EXT, 3 * BLK, LANES), f32),
                pltpu.VMEM((NSRC, EXT, EXT, GROUPS, LANES), f32),
                pltpu.VMEM((EXT, EXT, GROUPS, LANES), f32),
                pltpu.VMEM((EXT, EXT, GROUPS, LANES), f32),
                dma,
                dma((max(nx - 1, 1),)), dma((max(nx - 1, 1),)),
                dma((ZLO - 1,)), dma((ZLO - 1,)),
                dma((8,)), dma((8,)),
                dma((2, 8)), dma((2, 8)),
            ],
            compiler_params=pltpu.CompilerParams(collective_id=0, has_side_effects=True),
        )(src_owner, src_slot, orbitals)

    return jax.shard_map(
        body, mesh=mesh, in_specs=(P("sx", "sy", "orb"), P(), P()), out_specs=P("sx", "sy", "orb"), check_vma=False
    )
```

```python
import functools
import math

import jax
import jax.numpy as jnp
import numpy as np
from jax import lax
from jax.experimental import pallas as pl
from jax.experimental.pallas import tpu as pltpu
from jax.sharding import PartitionSpec as P

NZ = 32
NSRC = 4
ZLO = 3
LANES = 128
PACK = LANES // NZ
GROUPS = 8
HALO = 4
BLK = 8
EXT = BLK + 2 * HALO
MESH = pl.DeviceIdType.MESH

C = (1.021021021021021, -1.7357357357357357, 1.4753753753753753, -1.254069069069069, 1.0659587087087088)
IN_B = (C[0] - C[2] + C[4], C[1] - 3 * C[3], 2 * C[2] - 8 * C[4], 4 * C[3], 8 * C[4])
IN_S = tuple(a * (-1.0 / 6.0) ** k for k, a in enumerate(IN_B))
LEAD = IN_S[4]
REL = tuple(a / LEAD for a in IN_S)

UNROLL = 2
TERMS = 4


def constants():
    chain = np.eye(NZ, k=1) + np.eye(NZ, k=-1)
    q = []
    for m in range(TERMS):
        z = sum(math.comb(m + n, m) * REL[m + n] * np.linalg.matrix_power(chain, n) for n in range(5 - m))
        q.append(np.kron(np.eye(PACK), z))
    q = np.concatenate(q).astype(np.float32)
    high = q.astype(jnp.bfloat16)
    low = (q - high.astype(np.float32)).astype(jnp.bfloat16)
    same = np.tile(np.eye(NZ), (PACK, PACK))
    into = [same * (np.arange(LANES)[None] // NZ == s) for s in range(NSRC)]
    gather = np.concatenate(into).astype(jnp.bfloat16)
    spread = np.concatenate([one.T for one in into]).astype(jnp.bfloat16)
    return np.concatenate([high, low, gather, spread], axis=1)


DIRS = tuple((ax, ay) for ax in (-1, 0, 1) for ay in (-1, 0, 1) if (ax, ay) != (0, 0))


def src_range(a, width):
    return {-1: slice(HALO, HALO + width), 0: slice(HALO, HALO + BLK), 1: slice(HALO + BLK - width, HALO + BLK)}[a]


def dst_range(a, width):
    return {-1: slice(HALO + BLK, HALO + BLK + width), 0: slice(HALO, HALO + BLK), 1: slice(HALO - width, HALO)}[a]


def kernel(
    nx, nsx, nsy,
    owner, slot, orb_hbm, mats_hbm, out,
    inb, mats, tall, phi, gx, gz, pp, pt, rho, u1, u2, u3, u4, xh, xl, res,
    in_sem, mat_sem, xs, xr, zs, zr, ps, pr, hs, hr,
):
    orb = lax.axis_index("orb")
    mx, mz = orb // ZLO, orb % ZLO
    sx, sy = lax.axis_index("sx"), lax.axis_index("sy")

    def near(ax, ay):
        return {"sx": lax.rem(sx + ax + nsx, nsx), "sy": lax.rem(sy + ay + nsy, nsy)}

    def x_peer(d):
        return {"orb": lax.rem(mx + d, nx) * ZLO + mz}

    def z_peer(d):
        return {"orb": mx * ZLO + lax.rem(mz + d, ZLO)}

    load = pltpu.make_async_copy(orb_hbm, inb, in_sem)
    load.start()
    load_mats = pltpu.make_async_copy(mats_hbm, mats, mat_sem)
    load_mats.start()
    barrier = pltpu.get_barrier_semaphore()
    peers = [near(*d) for d in DIRS] + [x_peer(d) for d in range(1, nx)] + [z_peer(d) for d in range(1, ZLO)]
    for peer in peers:
        pl.semaphore_signal(barrier, inc=1, device_id=peer, device_id_type=MESH)
    load.wait()

    lane = lax.broadcasted_iota(jnp.int32, (BLK, LANES), 1)
    part = lane // NZ

    mine = part + orb * (2 * GROUPS * PACK)
    wanted = [owner[s // 2, s % 2] * (2 * GROUPS * PACK) + slot[s // 2, s % 2] for s in range(NSRC)]
    got = [jnp.zeros((BLK, BLK, LANES), jnp.float32) for s in range(NSRC)]
    for g in range(2 * GROUPS):
        row = inb[:, :, g * LANES : (g + 1) * LANES].astype(jnp.float32)
        for s in range(NSRC):
            got[s] = jnp.where((mine + g * PACK == wanted[s])[None], row, got[s])
    load_mats.wait()
    rows = jnp.concatenate([v.reshape(BLK * BLK, LANES).astype(jnp.bfloat16) for v in got], axis=1)
    cand = jnp.dot(rows, mats[:, 2 * LANES : 3 * LANES], preferred_element_type=jnp.float32)
    gx[mx] = cand.reshape(BLK, BLK, LANES).astype(jnp.bfloat16)

    def relay(x, carry):
        for g in range(2 * GROUPS):
            tall[x, pl.ds(g, BLK, stride=2 * GROUPS), :] = inb[x, :, g * LANES : (g + 1) * LANES].astype(jnp.float32)
        for h in range(2):
            for y in range(BLK):
                at = (2 * y + h) * GROUPS
                phi[h, HALO + x, HALO + y] = tall[x, at : at + GROUPS, :].astype(jnp.bfloat16)
        return carry

    lax.fori_loop(0, BLK, relay, 0)

    pl.semaphore_wait(barrier, len(peers))

    x_copies = [
        pltpu.make_async_remote_copy(gx.at[mx], gx.at[mx], xs.at[d - 1], xr.at[d - 1], device_id=x_peer(d), device_id_type=MESH)
        for d in range(1, nx)
    ]
    for copy in x_copies:
        copy.start()

    def halo_copies(h):
        copies = []
        for k, (ax, ay) in enumerate(DIRS):
            width = HALO - 1 if ax and ay else HALO
            copies.append(
                pltpu.make_async_remote_copy(
                    phi.at[h, src_range(ax, width), src_range(ay, width)],
                    phi.at[h, dst_range(ax, width), dst_range(ay, width)],
                    hs.at[h, k], hr.at[h, k], device_id=near(ax, ay), device_id_type=MESH,
                )
            )
        return copies

    first, second = halo_copies(0), halo_copies(1)
    for copy in first:
        copy.start()

    for copy in x_copies:
        copy.wait_recv()
    mid = gx[0].astype(jnp.float32)
    for x in range(1, nx):
        mid = mid + gx[x].astype(jnp.float32)
    gz[mz] = mid.astype(jnp.bfloat16)
    z_copies = [
        pltpu.make_async_remote_copy(gz.at[mz], gz.at[mz], zs.at[d - 1], zr.at[d - 1], device_id=z_peer(d), device_id_type=MESH)
        for d in range(1, ZLO)
    ]
    for copy in z_copies:
        copy.start()
    for copy in z_copies:
        copy.wait_recv()
    mid = gz[0].astype(jnp.float32)
    for z in range(1, ZLO):
        mid = mid + gz[z].astype(jnp.float32)
    pp[1, HALO : HALO + BLK] = mid.astype(jnp.bfloat16)
    p_copies = [
        pltpu.make_async_remote_copy(
            pp.at[1, src_range(ax, HALO)], pp.at[1 - ay, dst_range(ax, HALO)],
            ps.at[k], pr.at[k], device_id=near(ax, ay), device_id_type=MESH,
        )
        for k, (ax, ay) in enumerate(DIRS)
    ]
    for copy in p_copies:
        copy.start()
    for copy in second:
        copy.start()
    for copy in p_copies:
        copy.wait_recv()

    every = pp[...].astype(jnp.float32).reshape(3 * EXT * BLK, LANES).astype(jnp.bfloat16)
    for s in range(NSRC):
        wide = jnp.dot(every, mats[s * LANES : (s + 1) * LANES, 3 * LANES :], preferred_element_type=jnp.float32)
        wide = wide.reshape(3, EXT, BLK, LANES)
        for b in range(3):
            pt[s, :, b * BLK : (b + 1) * BLK, :] = wide[b]

    def level(k, src, dst):
        n = EXT - 2 * k
        rows = slice(k - 1, k + n + 1)
        inner = slice(k, k + n)

        def step(x, carry):
            diag, here = carry
            after = src[x + 1, rows]
            diag_here = here[: n + 1] + after[1:]
            dst[x, inner] = diag + diag_here[:n]
            return diag_here[1:], after

        here = src[k, rows]
        diag = src[k - 1, inner] + here[2:]
        lax.fori_loop(k, k + n, step, (diag, here), unroll=UNROLL)

    core = slice(HALO, HALO + BLK)
    plane = BLK * GROUPS

    def half(h):
        lo = h * GROUPS

        def density(x, carry):
            row = phi[h, x].astype(jnp.float32)
            for s in range(NSRC):
                for y in range(EXT):
                    rho[s, x, y] = row[y] * pt[s, x, y + HALO : y + HALO + 1, :]
            return carry

        lax.fori_loop(0, EXT, density, 0)

        def source(s, carry):
            level(1, rho.at[s], u1)
            level(2, u1, u2)
            level(3, u2, u3)
            level(4, u3, u4.at[s])

            def split(x, carry):
                at = pl.ds(pl.multiple_of(x * plane, plane), plane)
                for m, ref in enumerate((rho.at[s], u1, u2, u3)):
                    value = ref[HALO + x, core].reshape(plane, LANES)
                    high = value.astype(jnp.bfloat16)
                    xh[at, m * LANES : (m + 1) * LANES] = high
                    xl[at, m * LANES : (m + 1) * LANES] = (value - high.astype(jnp.float32)).astype(jnp.bfloat16)
                return carry

            lax.fori_loop(0, BLK, split, 0, unroll=2)
            both = jnp.dot(xh[...], mats[:, : 2 * LANES], preferred_element_type=jnp.float32)
            rest = jnp.dot(xl[...], mats[:, :LANES], preferred_element_type=jnp.float32)
            res[s] = both[:, :LANES] + both[:, LANES:] + rest
            return carry

        lax.fori_loop(0, NSRC, source, 0)

        def finish(x, carry):
            for y in range(BLK):
                total = jnp.zeros((GROUPS, LANES), jnp.float32)
                for s in range(NSRC):
                    at = pl.ds(pl.multiple_of(x * plane + y * GROUPS, GROUPS), GROUPS)
                    value = res[s, at, :] + u4[s, HALO + x, HALO + y]
                    total = total + value * pt[s, x + HALO, y + 2 * HALO : y + 2 * HALO + 1, :]
                at = (2 * y + h) * GROUPS
                tall[x, at : at + GROUPS, :] = total * (-LEAD)
            for g in range(lo, lo + GROUPS):
                out[x, :, g * LANES : (g + 1) * LANES] = tall[x, pl.ds(g, BLK, stride=2 * GROUPS), :]
            return carry

        lax.fori_loop(0, BLK, finish, 0)

    for copy in first:
        copy.wait_recv()
    half(0)
    for copy in second:
        copy.wait_recv()
    half(1)
    for copy in x_copies + z_copies + p_copies + first + second:
        copy.wait_send()


def solution(mesh):
    nx, nsx, nsy = mesh.shape["orb"] // ZLO, mesh.shape["sx"], mesh.shape["sy"]

    def body(orbitals, src_owner, src_slot):
        f32, bf16 = jnp.float32, jnp.bfloat16
        mats = constants()
        dma = pltpu.SemaphoreType.DMA
        return pl.pallas_call(
            functools.partial(kernel, nx, nsx, nsy),
            out_shape=jax.ShapeDtypeStruct(orbitals.shape, f32),
            in_specs=[
                pl.BlockSpec(memory_space=pltpu.SMEM),
                pl.BlockSpec(memory_space=pltpu.SMEM),
                pl.BlockSpec(memory_space=pl.ANY),
                pl.BlockSpec(memory_space=pl.ANY),
            ],
            out_specs=pl.BlockSpec(memory_space=pltpu.VMEM),
            scratch_shapes=[
                pltpu.VMEM(orbitals.shape, bf16),
                pltpu.VMEM(mats.shape, bf16),
                pltpu.VMEM((BLK, BLK * 2 * GROUPS, LANES), f32),
                pltpu.VMEM((2, EXT, EXT, GROUPS, LANES), bf16),
                pltpu.VMEM((nx, BLK, BLK, LANES), bf16),
                pltpu.VMEM((ZLO, BLK, BLK, LANES), bf16),
                pltpu.VMEM((3, EXT, BLK, LANES), bf16),
                pltpu.VMEM((NSRC, EXT, 3 * BLK, LANES), f32),
                pltpu.VMEM((NSRC, EXT, EXT, GROUPS, LANES), f32),
                pltpu.VMEM((EXT, EXT, GROUPS, LANES), f32),
                pltpu.VMEM((EXT, EXT, GROUPS, LANES), f32),
                pltpu.VMEM((EXT, EXT, GROUPS, LANES), f32),
                pltpu.VMEM((NSRC, EXT, EXT, GROUPS, LANES), f32),
                pltpu.VMEM((BLK * BLK * GROUPS, TERMS * LANES), bf16),
                pltpu.VMEM((BLK * BLK * GROUPS, TERMS * LANES), bf16),
                pltpu.VMEM((NSRC, BLK * BLK * GROUPS, LANES), f32),
                dma, dma,
                dma((max(nx - 1, 1),)), dma((max(nx - 1, 1),)),
                dma((ZLO - 1,)), dma((ZLO - 1,)),
                dma((8,)), dma((8,)),
                dma((2, 8)), dma((2, 8)),
            ],
            compiler_params=pltpu.CompilerParams(collective_id=0, has_side_effects=True),
        )(src_owner, src_slot, orbitals, jnp.asarray(mats))

    return jax.shard_map(
        body, mesh=mesh, in_specs=(P("sx", "sy", "orb"), P(), P()), out_specs=P("sx", "sy", "orb"), check_vma=False
    )
```

```python
import functools
import math

import jax
import jax.numpy as jnp
import numpy as np
from jax import lax
from jax.experimental import pallas as pl
from jax.experimental.pallas import tpu as pltpu
from jax.sharding import PartitionSpec as P

NZ = 32
NSRC = 4
LANES = 128
PACK = LANES // NZ
GROUPS = 8
HALO = 4
BLK = 8
EXT = BLK + 2 * HALO
MESH = pl.DeviceIdType.MESH

C = (1.021021021021021, -1.7357357357357357, 1.4753753753753753, -1.254069069069069, 1.0659587087087088)
IN_B = (C[0] - C[2] + C[4], C[1] - 3 * C[3], 2 * C[2] - 8 * C[4], 4 * C[3], 8 * C[4])
IN_S = tuple(a * (-1.0 / 6.0) ** k for k, a in enumerate(IN_B))
LEAD = IN_S[4]
REL = tuple(a / LEAD for a in IN_S)

UNROLL = 2
FIRST, REST = slice(0, None), slice(0, 0)
SPREAD = tuple((ax, ay) for ay in (-1, 1, 0) for ax in (0, -1, 1) if (ax, ay) != (0, 0))
TERMS = 4


def constants():
    chain = np.eye(NZ, k=1) + np.eye(NZ, k=-1)
    q = []
    for m in range(TERMS):
        z = sum(math.comb(m + n, m) * REL[m + n] * np.linalg.matrix_power(chain, n) for n in range(5 - m))
        q.append(np.kron(np.eye(PACK), z))
    q = np.concatenate(q).astype(np.float32)
    high = q.astype(jnp.bfloat16)
    low = (q - high.astype(np.float32)).astype(jnp.bfloat16)
    same = np.tile(np.eye(NZ), (PACK, PACK))
    into = [same * (np.arange(LANES)[None] // NZ == s) for s in range(NSRC)]
    gather = np.concatenate(into).astype(jnp.bfloat16)
    spread = np.concatenate([one.T for one in into]).astype(jnp.bfloat16)
    return np.concatenate([high, low, gather, spread], axis=1)


DIRS = tuple((ax, ay) for ax in (-1, 0, 1) for ay in (-1, 0, 1) if (ax, ay) != (0, 0))


def src_range(a, width):
    return {-1: slice(HALO, HALO + width), 0: slice(HALO, HALO + BLK), 1: slice(HALO + BLK - width, HALO + BLK)}[a]


def dst_range(a, width):
    return {-1: slice(HALO + BLK, HALO + BLK + width), 0: slice(HALO, HALO + BLK), 1: slice(HALO - width, HALO)}[a]


def kernel(
    norb, nsx, nsy,
    owner_hbm, slot_hbm, orb_hbm, mats_hbm, out,
    small, inb, mats, tall, phi, gx, pz, pt, rho, u1, u2, u3, u4, xh, xl, res,
    in_sem, mat_sem, small_sem, xs, xr, ps, pr, hs, hr,
):
    orb = lax.axis_index("orb")
    sx, sy = lax.axis_index("sx"), lax.axis_index("sy")

    def near(ax, ay):
        return {"sx": lax.rem(sx + ax + nsx, nsx), "sy": lax.rem(sy + ay + nsy, nsy)}

    def orb_peer(d):
        return {"orb": lax.rem(orb + d, norb)}

    barrier = pltpu.get_barrier_semaphore()
    peers = [near(*d) for d in SPREAD] + [orb_peer(d) for d in range(1, norb)]
    for peer in peers:
        pl.semaphore_signal(barrier, inc=1, device_id=peer, device_id_type=MESH)
    load = pltpu.make_async_copy(orb_hbm, inb, in_sem)
    load.start()
    load_mats = pltpu.make_async_copy(mats_hbm, mats, mat_sem)
    load_mats.start()
    load_owner = pltpu.make_async_copy(owner_hbm, small.at[0], small_sem.at[0])
    load_owner.start()
    load_slot = pltpu.make_async_copy(slot_hbm, small.at[1], small_sem.at[1])
    load_slot.start()
    load_owner.wait()
    load_slot.wait()
    load.wait()

    lane = lax.broadcasted_iota(jnp.int32, (BLK, LANES), 1)
    part = lane // NZ

    mine = part + orb * (2 * GROUPS * PACK)
    wanted = [small[0, s // 2, s % 2] * (2 * GROUPS * PACK) + small[1, s // 2, s % 2] for s in range(NSRC)]
    got = [jnp.zeros((BLK, BLK, LANES), jnp.float32) for s in range(NSRC)]
    for g in range(2 * GROUPS):
        row = inb[:, :, g * LANES : (g + 1) * LANES].astype(jnp.float32)
        for s in range(NSRC):
            got[s] = jnp.where((mine + g * PACK == wanted[s])[None], row, got[s])
    load_mats.wait()
    rows = jnp.concatenate([v.reshape(BLK * BLK, LANES).astype(jnp.bfloat16) for v in got], axis=1)
    cand = jnp.dot(rows, mats[:, 2 * LANES : 3 * LANES], preferred_element_type=jnp.float32)
    for x in range(BLK):
        tall[0, pl.ds(x, BLK, stride=BLK), :] = cand[x * BLK : (x + 1) * BLK]
    gx[orb] = tall[0, : BLK * BLK].reshape(BLK, BLK, LANES).astype(jnp.bfloat16)

    def relay(x, carry):
        for g in range(2 * GROUPS):
            tall[x, pl.ds(g, BLK, stride=2 * GROUPS), :] = inb[x, :, g * LANES : (g + 1) * LANES].astype(jnp.float32)
        for h in range(2):
            for y in range(BLK):
                at = (2 * y + h) * GROUPS
                phi[h, HALO + x, HALO + y] = tall[x, at : at + GROUPS, :].astype(jnp.bfloat16)
        return carry

    lax.fori_loop(0, BLK, relay, 0)

    pl.semaphore_wait(barrier, len(peers))

    x_copies = [
        pltpu.make_async_remote_copy(
            gx.at[orb], gx.at[orb], xs.at[d - 1], xr.at[d - 1], device_id=orb_peer(d), device_id_type=MESH
        )
        for d in range(1, norb)
    ]
    for copy in x_copies:
        copy.start()

    def halo_copies(h):
        copies = []
        for k, (ax, ay) in enumerate(DIRS):
            width = HALO - 1 if ax and ay else HALO
            copies.append(
                pltpu.make_async_remote_copy(
                    phi.at[h, src_range(ax, width), src_range(ay, width)],
                    phi.at[h, dst_range(ax, width), dst_range(ay, width)],
                    hs.at[h, k], hr.at[h, k], device_id=near(ax, ay), device_id_type=MESH,
                )
            )
        return copies

    first, second = halo_copies(0), halo_copies(1)
    for copy in first[FIRST]:
        copy.start()
    for copy in x_copies:
        copy.wait_recv()
    mid = gx[0].astype(jnp.float32)
    for x in range(1, norb):
        mid = mid + gx[x].astype(jnp.float32)
    pz[1, HALO : HALO + BLK] = mid.astype(jnp.bfloat16)
    p_copies = []
    for k, (ax, ay) in enumerate(SPREAD):
        width = HALO - 1 if ax and ay else HALO
        p_copies.append(
            pltpu.make_async_remote_copy(
                pz.at[1, src_range(ay, width)], pz.at[1 - ax, dst_range(ay, width)],
                ps.at[k], pr.at[k], device_id=near(ax, ay), device_id_type=MESH,
            )
        )
    for copy in p_copies:
        copy.start()
    for copy in first[REST]:
        copy.start()
    for copy in second:
        copy.start()
    for copy in p_copies:
        copy.wait_recv()

    every = pz[...].astype(jnp.float32)
    every = every.reshape(3 * EXT * BLK, LANES).astype(jnp.bfloat16)
    for s in range(NSRC):
        wide = jnp.dot(every, mats[s * LANES : (s + 1) * LANES, 3 * LANES :], preferred_element_type=jnp.float32)
        wide = wide.reshape(3, EXT, BLK, LANES)
        for b in range(3):
            pt[s, :, b * BLK : (b + 1) * BLK, :] = wide[b]

    def level(k, src, dst):
        n = EXT - 2 * k
        rows = slice(k - 1, k + n + 1)
        inner = slice(k, k + n)

        def step(x, carry):
            diag, here = carry
            after = src[x + 1, rows]
            diag_here = here[: n + 1] + after[1:]
            dst[x, inner] = diag + diag_here[:n]
            return diag_here[1:], after

        here = src[k, rows]
        diag = src[k - 1, inner] + here[2:]
        lax.fori_loop(k, k + n, step, (diag, here), unroll=UNROLL)

    core = slice(HALO, HALO + BLK)
    plane = BLK * GROUPS

    def half(h):
        lo = h * GROUPS

        def density(x, carry):
            row = phi[h, x].astype(jnp.float32)
            for s in range(NSRC):
                for y in range(EXT):
                    rho[s, x, y] = row[y] * pt[s, y, pl.ds(x + HALO, 1), :]
            return carry

        lax.fori_loop(0, EXT, density, 0)

        def source(s, carry):
            level(1, rho.at[s], u1)
            level(2, u1, u2)
            level(3, u2, u3)
            level(4, u3, u4.at[s])

            def split(x, carry):
                at = pl.ds(pl.multiple_of(x * plane, plane), plane)
                for m, ref in enumerate((rho.at[s], u1, u2, u3)):
                    value = ref[HALO + x, core].reshape(plane, LANES)
                    high = value.astype(jnp.bfloat16)
                    xh[s, at, m * LANES : (m + 1) * LANES] = high
                    xl[s, at, m * LANES : (m + 1) * LANES] = (value - high.astype(jnp.float32)).astype(jnp.bfloat16)
                return carry

            lax.fori_loop(0, BLK, split, 0, unroll=2)
            return carry

        lax.fori_loop(0, NSRC, source, 0)
        every_row = (NSRC * BLK * plane, TERMS * LANES)
        both = jnp.dot(xh[...].reshape(every_row), mats[:, : 2 * LANES], preferred_element_type=jnp.float32)
        rest = jnp.dot(xl[...].reshape(every_row), mats[:, :LANES], preferred_element_type=jnp.float32)
        res[...] = (both[:, :LANES] + both[:, LANES:] + rest).reshape(NSRC, BLK * plane, LANES)

        def finish(x, carry):
            for y in range(BLK):
                total = jnp.zeros((GROUPS, LANES), jnp.float32)
                for s in range(NSRC):
                    at = pl.ds(pl.multiple_of(x * plane + y * GROUPS, GROUPS), GROUPS)
                    value = res[s, at, :] + u4[s, HALO + x, HALO + y]
                    total = total + value * pt[s, y + HALO, pl.ds(x + 2 * HALO, 1), :]
                at = (2 * y + h) * GROUPS
                tall[x, at : at + GROUPS, :] = total * (-LEAD)
            for g in range(lo, lo + GROUPS):
                out[x, :, g * LANES : (g + 1) * LANES] = tall[x, pl.ds(g, BLK, stride=2 * GROUPS), :]
            return carry

        lax.fori_loop(0, BLK, finish, 0)

    for copy in first:
        copy.wait_recv()
    half(0)
    for copy in second:
        copy.wait_recv()
    half(1)
    for copy in x_copies + p_copies + first + second:
        copy.wait_send()


def solution(mesh):
    norb, nsx, nsy = mesh.shape["orb"], mesh.shape["sx"], mesh.shape["sy"]

    def body(orbitals, src_owner, src_slot):
        f32, bf16 = jnp.float32, jnp.bfloat16
        mats = constants()
        dma = pltpu.SemaphoreType.DMA
        return pl.pallas_call(
            functools.partial(kernel, norb, nsx, nsy),
            out_shape=jax.ShapeDtypeStruct(orbitals.shape, f32),
            in_specs=[
                pl.BlockSpec(memory_space=pl.ANY),
                pl.BlockSpec(memory_space=pl.ANY),
                pl.BlockSpec(memory_space=pl.ANY),
                pl.BlockSpec(memory_space=pl.ANY),
            ],
            out_specs=pl.BlockSpec(memory_space=pltpu.VMEM),
            scratch_shapes=[
                pltpu.SMEM((2,) + src_owner.shape, jnp.int32),
                pltpu.VMEM(orbitals.shape, bf16),
                pltpu.VMEM(mats.shape, bf16),
                pltpu.VMEM((BLK, BLK * 2 * GROUPS, LANES), f32),
                pltpu.VMEM((2, EXT, EXT, GROUPS, LANES), bf16),
                pltpu.VMEM((norb, BLK, BLK, LANES), bf16),
                pltpu.VMEM((3, EXT, BLK, LANES), bf16),
                pltpu.VMEM((NSRC, EXT, 3 * BLK, LANES), f32),
                pltpu.VMEM((NSRC, EXT, EXT, GROUPS, LANES), f32),
                pltpu.VMEM((EXT, EXT, GROUPS, LANES), f32),
                pltpu.VMEM((EXT, EXT, GROUPS, LANES), f32),
                pltpu.VMEM((EXT, EXT, GROUPS, LANES), f32),
                pltpu.VMEM((NSRC, EXT, EXT, GROUPS, LANES), f32),
                pltpu.VMEM((NSRC, BLK * BLK * GROUPS, TERMS * LANES), bf16),
                pltpu.VMEM((NSRC, BLK * BLK * GROUPS, TERMS * LANES), bf16),
                pltpu.VMEM((NSRC, BLK * BLK * GROUPS, LANES), f32),
                dma, dma, dma((2,)),
                dma((norb - 1,)), dma((norb - 1,)),
                dma((len(SPREAD),)), dma((len(SPREAD),)),
                dma((2, 8)), dma((2, 8)),
            ],
            compiler_params=pltpu.CompilerParams(collective_id=0, has_side_effects=True),
        )(src_owner, src_slot, orbitals, jnp.asarray(mats))

    return jax.shard_map(
        body, mesh=mesh, in_specs=(P("sx", "sy", "orb"), P(), P()), out_specs=P("sx", "sy", "orb"), check_vma=False
    )
```

```python
import functools
import math

import jax
import jax.numpy as jnp
import numpy as np
from jax import lax
from jax.experimental import pallas as pl
from jax.experimental.pallas import tpu as pltpu
from jax.sharding import PartitionSpec as P

NZ = 32
NSRC = 4
LANES = 128
PACK = LANES // NZ
GROUPS = 8
HALO = 4
BLK = 8
EXT = BLK + 2 * HALO
MESH = pl.DeviceIdType.MESH

C = (1.021021021021021, -1.7357357357357357, 1.4753753753753753, -1.254069069069069, 1.0659587087087088)
IN_B = (C[0] - C[2] + C[4], C[1] - 3 * C[3], 2 * C[2] - 8 * C[4], 4 * C[3], 8 * C[4])
IN_S = tuple(a * (-1.0 / 6.0) ** k for k, a in enumerate(IN_B))
LEAD = IN_S[4]
REL = tuple(a / LEAD for a in IN_S)

UNROLL = 2
FIRST, REST = slice(0, None), slice(0, 0)
SPREAD = tuple((ax, ay) for ay in (-1, 1, 0) for ax in (0, -1, 1) if (ax, ay) != (0, 0))
TERMS = 4


def constants():
    chain = np.eye(NZ, k=1) + np.eye(NZ, k=-1)
    q = []
    for m in range(TERMS):
        z = sum(math.comb(m + n, m) * REL[m + n] * np.linalg.matrix_power(chain, n) for n in range(5 - m))
        q.append(np.kron(np.eye(PACK), z))
    q = np.concatenate(q).astype(np.float32)
    high = q.astype(jnp.bfloat16)
    low = (q - high.astype(np.float32)).astype(jnp.bfloat16)
    same = np.tile(np.eye(NZ), (PACK, PACK))
    into = [same * (np.arange(LANES)[None] // NZ == s) for s in range(NSRC)]
    gather = np.concatenate(into).astype(jnp.bfloat16)
    spread = np.concatenate([one.T for one in into]).astype(jnp.bfloat16)
    return np.concatenate([high, low, gather, spread], axis=1)


DIRS = tuple((ax, ay) for ax in (-1, 0, 1) for ay in (-1, 0, 1) if (ax, ay) != (0, 0))


def src_range(a, width):
    return {-1: slice(HALO, HALO + width), 0: slice(HALO, HALO + BLK), 1: slice(HALO + BLK - width, HALO + BLK)}[a]


def dst_range(a, width):
    return {-1: slice(HALO + BLK, HALO + BLK + width), 0: slice(HALO, HALO + BLK), 1: slice(HALO - width, HALO)}[a]


def kernel(
    norb, nsx, nsy,
    owner_hbm, slot_hbm, orb_hbm, mats_hbm, out,
    small, inb, mats, tall, phi, gx, pz, pt, rho, u1, u2, u3, u4, xh, xl, res,
    in_sem, mat_sem, small_sem, xs, xr, ps, pr, hs, hr,
):
    orb = lax.axis_index("orb")
    sx, sy = lax.axis_index("sx"), lax.axis_index("sy")

    def near(ax, ay):
        return {"sx": lax.rem(sx + ax + nsx, nsx), "sy": lax.rem(sy + ay + nsy, nsy)}

    def orb_peer(d):
        return {"orb": lax.rem(orb + d, norb)}

    barrier = pltpu.get_barrier_semaphore()
    peers = [near(*d) for d in SPREAD] + [orb_peer(d) for d in range(1, norb)]
    for peer in peers:
        pl.semaphore_signal(barrier, inc=1, device_id=peer, device_id_type=MESH)
    load = pltpu.make_async_copy(orb_hbm, inb, in_sem)
    load.start()
    load_mats = pltpu.make_async_copy(mats_hbm, mats, mat_sem)
    load_mats.start()
    load_owner = pltpu.make_async_copy(owner_hbm, small.at[0], small_sem.at[0])
    load_owner.start()
    load_slot = pltpu.make_async_copy(slot_hbm, small.at[1], small_sem.at[1])
    load_slot.start()
    load_owner.wait()
    load_slot.wait()
    load.wait()

    lane = lax.broadcasted_iota(jnp.int32, (BLK, LANES), 1)
    part = lane // NZ

    mine = part + orb * (2 * GROUPS * PACK)
    wanted = [small[0, s // 2, s % 2] * (2 * GROUPS * PACK) + small[1, s // 2, s % 2] for s in range(NSRC)]
    got = [jnp.zeros((BLK, BLK, LANES), jnp.float32) for s in range(NSRC)]
    for g in range(2 * GROUPS):
        row = inb[:, :, g * LANES : (g + 1) * LANES].astype(jnp.float32)
        for s in range(NSRC):
            got[s] = jnp.where((mine + g * PACK == wanted[s])[None], row, got[s])
    load_mats.wait()
    rows = jnp.concatenate([v.reshape(BLK * BLK, LANES).astype(jnp.bfloat16) for v in got], axis=1)
    cand = jnp.dot(rows, mats[:, 2 * LANES : 3 * LANES], preferred_element_type=jnp.float32)
    for x in range(BLK):
        tall[0, pl.ds(x, BLK, stride=BLK), :] = cand[x * BLK : (x + 1) * BLK]
    gx[orb] = tall[0, : BLK * BLK].reshape(BLK, BLK, LANES).astype(jnp.bfloat16)

    def relay(x, carry):
        for g in range(2 * GROUPS):
            tall[x, pl.ds(g, BLK, stride=2 * GROUPS), :] = inb[x, :, g * LANES : (g + 1) * LANES].astype(jnp.float32)
        for h in range(2):
            for y in range(BLK):
                at = (2 * y + h) * GROUPS
                phi[h, HALO + x, HALO + y] = tall[x, at : at + GROUPS, :].astype(jnp.bfloat16)
        return carry

    lax.fori_loop(0, BLK, relay, 0)

    pl.semaphore_wait(barrier, len(peers))

    x_copies = [
        pltpu.make_async_remote_copy(
            gx.at[orb], gx.at[orb], xs.at[d - 1], xr.at[d - 1], device_id=orb_peer(d), device_id_type=MESH
        )
        for d in range(1, norb)
    ]
    for copy in x_copies:
        copy.start()

    def halo_copies(h):
        copies = []
        for k, (ax, ay) in enumerate(DIRS):
            width = HALO - 1 if ax and ay else HALO
            copies.append(
                pltpu.make_async_remote_copy(
                    phi.at[h, src_range(ax, width), src_range(ay, width)],
                    phi.at[h, dst_range(ax, width), dst_range(ay, width)],
                    hs.at[h, k], hr.at[h, k], device_id=near(ax, ay), device_id_type=MESH,
                )
            )
        return copies

    first, second = halo_copies(0), halo_copies(1)
    for copy in first[FIRST]:
        copy.start()
    for copy in x_copies:
        copy.wait_recv()
    mid = gx[0].astype(jnp.float32)
    for x in range(1, norb):
        mid = mid + gx[x].astype(jnp.float32)
    pz[1, HALO : HALO + BLK] = mid.astype(jnp.bfloat16)
    p_copies = []
    for k, (ax, ay) in enumerate(SPREAD):
        width = HALO - 1 if ax and ay else HALO
        p_copies.append(
            pltpu.make_async_remote_copy(
                pz.at[1, src_range(ay, width)], pz.at[1 - ax, dst_range(ay, width)],
                ps.at[k], pr.at[k], device_id=near(ax, ay), device_id_type=MESH,
            )
        )
    for copy in p_copies:
        copy.start()
    for copy in first[REST]:
        copy.start()
    for copy in second:
        copy.start()
    for copy in p_copies:
        copy.wait_recv()

    every = pz[...].astype(jnp.float32)
    every = every.reshape(3 * EXT * BLK, LANES).astype(jnp.bfloat16)
    for s in range(NSRC):
        wide = jnp.dot(every, mats[s * LANES : (s + 1) * LANES, 3 * LANES :], preferred_element_type=jnp.float32)
        wide = wide.reshape(3, EXT, BLK, LANES)
        for b in range(3):
            pt[s, :, b * BLK : (b + 1) * BLK, :] = wide[b]

    def level(k, src, dst):
        n = EXT - 2 * k
        rows = slice(k - 1, k + n + 1)
        inner = slice(k, k + n)

        def step(x, carry):
            diag, here = carry
            after = src[x + 1, rows]
            diag_here = here[: n + 1] + after[1:]
            dst[x, inner] = diag + diag_here[:n]
            return diag_here[1:], after

        here = src[k, rows]
        diag = src[k - 1, inner] + here[2:]
        lax.fori_loop(k, k + n, step, (diag, here), unroll=n)

    core = slice(HALO, HALO + BLK)
    plane = BLK * GROUPS

    def product(s):
        both = jnp.dot(xh[s], mats[:, : 2 * LANES], preferred_element_type=jnp.float32)
        rest = jnp.dot(xl[s], mats[:, :LANES], preferred_element_type=jnp.float32)
        res[s] = both[:, :LANES] + both[:, LANES:] + rest

    def half(h):
        lo = h * GROUPS

        def density(x, carry):
            row = phi[h, x].astype(jnp.float32)
            for s in range(NSRC):
                for y in range(EXT):
                    rho[s, x, y] = row[y] * pt[s, y, pl.ds(x + HALO, 1), :]
            return carry

        lax.fori_loop(0, EXT, density, 0, unroll=2)

        for s in range(NSRC):
            level(1, rho.at[s], u1)
            level(2, u1, u2)
            level(3, u2, u3)
            level(4, u3, u4.at[s])
            if s:
                product(s - 1)

            def split(x, carry):
                at = pl.ds(pl.multiple_of(x * plane, plane), plane)
                for m, ref in enumerate((rho.at[s], u1, u2, u3)):
                    value = ref[HALO + x, core].reshape(plane, LANES)
                    high = value.astype(jnp.bfloat16)
                    xh[s, at, m * LANES : (m + 1) * LANES] = high
                    xl[s, at, m * LANES : (m + 1) * LANES] = (value - high.astype(jnp.float32)).astype(jnp.bfloat16)
                return carry

            lax.fori_loop(0, BLK, split, 0, unroll=BLK)
        product(NSRC - 1)

        def finish(x, carry):
            for y in range(BLK):
                total = jnp.zeros((GROUPS, LANES), jnp.float32)
                for s in range(NSRC):
                    at = pl.ds(pl.multiple_of(x * plane + y * GROUPS, GROUPS), GROUPS)
                    value = res[s, at, :] + u4[s, HALO + x, HALO + y]
                    total = total + value * pt[s, y + HALO, pl.ds(x + 2 * HALO, 1), :]
                at = (2 * y + h) * GROUPS
                tall[x, at : at + GROUPS, :] = total * (-LEAD)
            for g in range(lo, lo + GROUPS):
                out[x, :, g * LANES : (g + 1) * LANES] = tall[x, pl.ds(g, BLK, stride=2 * GROUPS), :]
            return carry

        lax.fori_loop(0, BLK, finish, 0, unroll=2)

    for copy in first:
        copy.wait_recv()
    half(0)
    for copy in second:
        copy.wait_recv()
    half(1)
    for copy in x_copies + p_copies + first + second:
        copy.wait_send()


def solution(mesh):
    norb, nsx, nsy = mesh.shape["orb"], mesh.shape["sx"], mesh.shape["sy"]

    def body(orbitals, src_owner, src_slot):
        f32, bf16 = jnp.float32, jnp.bfloat16
        mats = constants()
        dma = pltpu.SemaphoreType.DMA
        return pl.pallas_call(
            functools.partial(kernel, norb, nsx, nsy),
            out_shape=pltpu.VMEM(orbitals.shape, f32),
            in_specs=[
                pl.BlockSpec(memory_space=pl.ANY),
                pl.BlockSpec(memory_space=pl.ANY),
                pl.BlockSpec(memory_space=pl.ANY),
                pl.BlockSpec(memory_space=pl.ANY),
            ],
            out_specs=pl.BlockSpec(memory_space=pltpu.VMEM),
            scratch_shapes=[
                pltpu.SMEM((2,) + src_owner.shape, jnp.int32),
                pltpu.VMEM(orbitals.shape, bf16),
                pltpu.VMEM(mats.shape, bf16),
                pltpu.VMEM((BLK, BLK * 2 * GROUPS, LANES), f32),
                pltpu.VMEM((2, EXT, EXT, GROUPS, LANES), bf16),
                pltpu.VMEM((norb, BLK, BLK, LANES), bf16),
                pltpu.VMEM((3, EXT, BLK, LANES), bf16),
                pltpu.VMEM((NSRC, EXT, 3 * BLK, LANES), f32),
                pltpu.VMEM((NSRC, EXT, EXT, GROUPS, LANES), f32),
                pltpu.VMEM((EXT, EXT, GROUPS, LANES), f32),
                pltpu.VMEM((EXT, EXT, GROUPS, LANES), f32),
                pltpu.VMEM((EXT, EXT, GROUPS, LANES), f32),
                pltpu.VMEM((NSRC, EXT, EXT, GROUPS, LANES), f32),
                pltpu.VMEM((NSRC, BLK * BLK * GROUPS, TERMS * LANES), bf16),
                pltpu.VMEM((NSRC, BLK * BLK * GROUPS, TERMS * LANES), bf16),
                pltpu.VMEM((NSRC, BLK * BLK * GROUPS, LANES), f32),
                dma, dma, dma((2,)),
                dma((norb - 1,)), dma((norb - 1,)),
                dma((len(SPREAD),)), dma((len(SPREAD),)),
                dma((2, 8)), dma((2, 8)),
            ],
            compiler_params=pltpu.CompilerParams(collective_id=0, has_side_effects=True),
        )(src_owner, src_slot, orbitals, jnp.asarray(mats))

    return jax.shard_map(
        body, mesh=mesh, in_specs=(P("sx", "sy", "orb"), P(), P()), out_specs=P("sx", "sy", "orb"), check_vma=False
    )
```
